512 devices in a mesh: leaf: 128 (over z, y, core), level: 4 (over x).
Axes of the slice: x: 4, y: 4, z: 16, core: 2. Of those that a mesh axis runs over, the one named last changes fastest.
Arguments:
- points_x: bfloat16 [256, 262144], P(None, ('leaf', 'level')), may hold values from -6 to 6
- leaf_basis: bfloat16 [512, 512, 256], P(('leaf', 'level')), may hold values from -0.25 to 0.25
- near_tiles: bfloat16 [512, 4, 512, 512], P(('leaf', 'level')), may hold values from -0.25 to 0.25
- near_cols: int32 [512, 4], P(('leaf', 'level')), may hold values from 0 to 11, as said below
- near_count: int32 [512], P(('leaf', 'level')), may hold values from 3 to 4, as said below
- transfer: bfloat16 [2, 256, 256], replicated, may hold values from -0.3125 to 0.3125
- coupling: bfloat16 [6, 2, 256, 256], replicated, may hold values from -0.375 to 0.375
- couple_mask: int32 [6, 128, 2], replicated, may hold values 0 or 1
Outputs:
- kernel_product: bfloat16 [256, 262144], P(None, ('leaf', 'level'))
The draws below stay inside these ranges and needn't reach their ends.
Inputs may be any that keep to these rules, and one draw needn't show every extreme that they name: Slots 0, 1 and 2 of leaf L name L itself, L - 1 and L + 1 (near_cols 4 + L mod 4, one less, one more); slot 3 names any leaf of the previous, own or next group; some leaf's slot 3 names 0 and some names 11. The live slots of a leaf are its first near_count slots; in every draw some leaf has 3 and some has 4 live slots.
All inputs are finite; a program needn't handle non-finite values.
Results may differ from the reference program's by a relative error of at most 0.015.
Values may be sent and summed in bfloat16 or wider, within the bound.
A program may use at most 64 MiB of HBM per device.

```python
import jax
import jax.numpy as jnp
from jax import lax

LEAF_PTS = 512
RANK = 256
VECS = 256
NEAR_SLOTS = 4
LEVELS = 6
GROUPS = 128
NLEAF = 512
NPTS = 262144
N_LEAF = 128
N_LEVEL = 4


def draw_near_count(key, part):
    key_busy, key_forced = jax.random.split(jax.random.fold_in(key, 17), 2)
    busy_flag = jax.random.randint(key_busy, (NLEAF,), 0, 5) == 0
    tile_count = jnp.where(busy_flag, NEAR_SLOTS, 3)
    forced_at = jax.random.randint(key_forced, (), 0, NLEAF)
    tile_count = tile_count.at[forced_at].set(NEAR_SLOTS)
    tile_count = tile_count.at[(forced_at + NLEAF // 2) % NLEAF].set(3)
    return tile_count.astype(jnp.int32)


def draw_near_cols(key, part):
    key_extra, key_forced = jax.random.split(jax.random.fold_in(key, 29), 2)
    leaf_ids = jnp.arange(NLEAF, dtype=jnp.int32)
    own_col = N_LEVEL + leaf_ids % N_LEVEL
    extra = jax.random.randint(key_extra, (NLEAF,), 0, 3 * N_LEVEL)
    forced_at = jax.random.randint(key_forced, (), 0, NLEAF)
    extra = extra.at[forced_at].set(0)
    extra = extra.at[(forced_at + NLEAF // 2) % NLEAF].set(3 * N_LEVEL - 1)
    return jnp.stack([own_col, own_col - 1, own_col + 1, extra], axis=1).astype(jnp.int32)


def set_ends(result, rng, smallest, top_value):
    longest = result.shape.index(max(result.shape))
    spots = []
    for shift in (0, 1):
        where = [jax.random.randint(jax.random.fold_in(rng, axis), (), 0, length) for axis, length in enumerate(result.shape)]
        where[longest] = (where[longest] + shift) % result.shape[longest]
        spots.append(tuple(where))
    return result.at[spots[0]].set(smallest).at[spots[1]].set(top_value)


def levels(key, dims, cuts, least, top_value):
    level, own = 1.0, jax.random.fold_in(key, 6)
    for dim, parts in cuts:
        steps = jnp.exp(jax.random.uniform(jax.random.fold_in(own, dim), (parts,), jnp.float32, least / len(cuts), top_value / len(cuts)))
        level = level * jnp.repeat(steps, dims[dim] // parts).reshape([-1 if axis == dim else 1 for axis in range(len(dims))])
    return level


def noise(stream_key, shape, width, reach, cuts=(), kind=jnp.bfloat16):
    drawn = width * jax.random.normal(stream_key, shape, jnp.float32)
    if cuts:
        drawn = drawn * levels(stream_key, shape, cuts, -0.22, 0.18)
    return jnp.clip(drawn, -reach, reach).astype(kind)


def setup_inputs(seed: int = 0) -> dict:
    splits = jax.random.split(jax.random.key(seed), 9)
    return {
        "points_x": noise(splits[0], (VECS, NPTS), 1.0, 6.0, ((1, 512),)),
        "leaf_basis": noise(splits[1], (NLEAF, LEAF_PTS, RANK), LEAF_PTS ** -0.5, 0.25, ((0, 512),)),
        "near_tiles": noise(splits[2], (NLEAF, NEAR_SLOTS, LEAF_PTS, LEAF_PTS), LEAF_PTS ** -0.5, 0.25, ((0, 512),)),
        "near_cols": draw_near_cols(jax.random.fold_in(splits[8], 71), 0),
        "near_count": draw_near_count(jax.random.fold_in(splits[8], 71), 0),
        "transfer": noise(splits[5], (2, RANK, RANK), (RANK * 3 // 2) ** -0.5, 0.3125),
        "coupling": noise(splits[6], (LEVELS, 2, RANK, RANK), RANK ** -0.5, 0.375),
        "couple_mask": set_ends((jax.random.randint(splits[7], (LEVELS, GROUPS, 2), 0, 2) < 1).astype(jnp.int32), jax.random.fold_in(splits[7], 1), 0, 1),
    }


def pair_up(coefs, transfer):
    lower_coef = coefs[0::2].astype(jnp.float32)
    upper_coef = coefs[1::2].astype(jnp.float32)
    summed = jnp.einsum("kvr,rs->kvs", lower_coef, transfer[0].astype(jnp.float32))
    summed = summed + jnp.einsum("kvr,rs->kvs", upper_coef, transfer[1].astype(jnp.float32))
    return summed.astype(jnp.bfloat16)


def split_down(fields, transfer):
    parent = fields.astype(jnp.float32)
    toward_lower = jnp.einsum("kvs,rs->kvr", parent, transfer[0].astype(jnp.float32))
    toward_upper = jnp.einsum("kvs,rs->kvr", parent, transfer[1].astype(jnp.float32))
    stacked = jnp.stack([toward_lower, toward_upper], axis=1)
    return stacked.reshape((2 * fields.shape[0],) + fields.shape[1:])


def couple_level(coefs, matrices, mask_rows):
    cluster_count = coefs.shape[0]
    coupled = jnp.zeros(coefs.shape, jnp.float32)
    wide_coefs = coefs.astype(jnp.float32)
    for pick_idx, offset in enumerate((2, 3)):
        if offset < cluster_count:
            matrix = matrices[pick_idx].astype(jnp.float32)
            zero_pad = jnp.zeros((offset,) + coefs.shape[1:], jnp.float32)
            ahead_coef = jnp.concatenate([wide_coefs[offset:], zero_pad], axis=0)
            behind = jnp.concatenate([zero_pad, wide_coefs[:cluster_count - offset]], axis=0)
            ahead_mask = mask_rows[:cluster_count, pick_idx].astype(jnp.float32)
            behind_mask = jnp.concatenate([jnp.zeros((offset,), jnp.float32), mask_rows[:cluster_count - offset, pick_idx].astype(jnp.float32)])
            coupled = coupled + ahead_mask[:, None, None] * jnp.einsum("kvr,rs->kvs", ahead_coef, matrix)
            coupled = coupled + behind_mask[:, None, None] * jnp.einsum("kvs,rs->kvr", behind, matrix)
    return coupled


def reference(points_x, leaf_basis, near_tiles, near_cols, near_count, transfer, coupling, couple_mask):
    vectors = points_x.shape[0]
    leaves = leaf_basis.shape[0]
    points = leaf_basis.shape[1]
    by_leaf = points_x.reshape(vectors, leaves, points).transpose(1, 0, 2)

    def leaf_coef(operands):
        return jnp.dot(operands[0], operands[1], preferred_element_type=jnp.float32).astype(jnp.bfloat16)

    level_coefs = lax.map(leaf_coef, (by_leaf, leaf_basis))
    group_bits = N_LEVEL.bit_length() - 1
    leaf_bits = N_LEAF.bit_length() - 1
    active = min(LEVELS, leaf_bits + 1)
    for step_idx in range(group_bits):
        level_coefs = pair_up(level_coefs, transfer)
    coarse = [level_coefs]
    for level_idx in range(1, active):
        coarse.append(pair_up(coarse[-1], transfer))
    couplings = [couple_level(coarse[level_idx], coupling[level_idx], couple_mask[level_idx]) for level_idx in range(active)]
    fields = couplings[active - 1].astype(jnp.bfloat16)
    for level_idx in range(active - 2, -1, -1):
        fields = (split_down(fields, transfer) + couplings[level_idx]).astype(jnp.bfloat16)
    for step_idx in range(group_bits):
        fields = split_down(fields, transfer).astype(jnp.bfloat16)

    group_width = N_LEVEL * points
    padded_x = jnp.pad(points_x, ((0, 0), (group_width, group_width)))

    def finish(leaf_items):
        tile_set, columns, tile_count, fields_leaf, leaf_map, leaf_id = leaf_items
        window_start = (leaf_id // N_LEVEL) * group_width
        window_x = lax.dynamic_slice_in_dim(padded_x, window_start.astype(jnp.int32), 3 * group_width, 1)
        running_sum = jnp.dot(fields_leaf, leaf_map.T, preferred_element_type=jnp.float32)
        for slot_idx in range(NEAR_SLOTS):
            column_x = lax.dynamic_slice_in_dim(window_x, (columns[slot_idx] * points).astype(jnp.int32), points, 1)
            tile_block = tile_set[slot_idx]
            running_sum = lax.cond(slot_idx < tile_count,
                                   lambda running: running + jnp.dot(column_x, tile_block, preferred_element_type=jnp.float32),
                                   lambda running: running, running_sum)
        return running_sum.astype(jnp.bfloat16)

    leaf_ids = jnp.arange(leaves, dtype=jnp.int32)
    blocks = lax.map(finish, (near_tiles, near_cols, near_count, fields, leaf_basis, leaf_ids))
    return blocks.transpose(1, 0, 2).reshape(vectors, leaves * points)
```

```python
import functools

import jax
import jax.numpy as jnp
from jax import lax
from jax.experimental import pallas as pl
from jax.experimental.pallas import tpu as pltpu
from jax.sharding import PartitionSpec as P

MESH = pl.DeviceIdType.MESH
F32, BF16 = jnp.float32, jnp.bfloat16

PLANE = 8
MEMBERS = 4
PEERS = PLANE * MEMBERS
DEPTH = 16
ROWS = 8


def reversed_bits(value, bits):
    out = 0
    for bit in range(bits):
        out = out + ((value // (1 << bit)) % 2) * (1 << (bits - 1 - bit))
    return out


def flat(blocks):
    wide = blocks.astype(F32)
    return wide.reshape(wide.shape[0] * wide.shape[1], wide.shape[2])


def mul(rows, matrix):
    return jnp.dot(rows.astype(BF16), matrix, preferred_element_type=F32)


def mul_t(rows, matrix):
    return lax.dot_general(
        rows.astype(BF16), matrix, (((1,), (1,)), ((), ())), preferred_element_type=F32
    )


def rounded(rows):
    return rows.astype(BF16).astype(F32)


def kernel(
    x_hbm, basis_hbm, tiles_hbm, transfer_hbm, coupling_hbm, cols_ref, count_ref, mask_ref,
    out_ref,
    win, basis, tiles, trans, coup, cbuf, abuf, tree, near_z, quad_z, planes, lev4, lev5, fbuf, gbuf, acc,
    load_sem, a_send, a_recv, z_send, z_recv, d_send, d_recv, n_send, n_recv,
):
    g = lax.axis_index("leaf")
    x = lax.axis_index("level")
    z = g // PLANE
    gp = g % PLANE
    core = g % 2
    base_g = g - gp
    me = gp * MEMBERS + x
    partner_g = g + 1 - 2 * core
    beyond_g = (g + 2 * core - 1 + PLANE * DEPTH) % (PLANE * DEPTH)
    x_up, x_down = (x + 1) % MEMBERS, (x + 3) % MEMBERS

    def load(k, src, dst):
        return pltpu.make_async_copy(src, dst, load_sem.at[k])

    loads = [
        load(0, x_hbm, win.at[4 + x]),
        load(1, basis_hbm, basis),
        load(2, transfer_hbm, trans),
        load(3, tiles_hbm, tiles),
        load(4, coupling_hbm, coup),
    ]
    for item in loads:
        item.start()

    barrier = pltpu.get_barrier_semaphore()

    def greet(j, carry):
        other = (me + j) % PEERS
        pl.semaphore_signal(
            barrier, inc=1, device_id=(base_g + other // MEMBERS, other % MEMBERS), device_id_type=MESH
        )
        return carry

    lax.fori_loop(1, PEERS, greet, 0)

    def greet_z(j, carry):
        pl.semaphore_signal(
            barrier, inc=1, device_id=(((z + j) % DEPTH) * PLANE + gp, x), device_id_type=MESH
        )
        return carry

    lax.fori_loop(1, DEPTH, greet_z, 0)
    pl.semaphore_signal(barrier, inc=1, device_id=(beyond_g, x), device_id_type=MESH)

    loads[0].wait()
    loads[1].wait()
    coef = jnp.dot(win[4 + x], basis[0], preferred_element_type=F32)
    cbuf[...] = coef.reshape(PEERS, ROWS, coef.shape[1]).astype(BF16)

    pl.semaphore_wait(barrier, PEERS - 1 + DEPTH - 1 + 1)

    my_slot = reversed_bits(me, 5)

    def send_a(j, carry):
        other = (me + j) % PEERS
        pltpu.make_async_remote_copy(
            src_ref=cbuf.at[other],
            dst_ref=abuf.at[my_slot],
            send_sem=a_send,
            recv_sem=a_recv,
            device_id=(base_g + other // MEMBERS, other % MEMBERS),
            device_id_type=MESH,
        ).start()
        return carry

    lax.fori_loop(1, PEERS, send_a, 0)
    pltpu.make_async_copy(cbuf.at[me], abuf.at[my_slot], a_recv).start()

    own = win.at[4 + x]

    def near_copy(src, dst, where, k):
        return pltpu.make_async_remote_copy(
            src_ref=src, dst_ref=dst, send_sem=n_send, recv_sem=n_recv.at[k],
            device_id=where, device_id_type=MESH,
        )

    near_copy(own, win.at[4 + x], (g, x_up), 0).start()
    near_copy(own, win.at[4 + x], (g, x_down), 1).start()

    def pass_on(member):
        near_copy(win.at[4 + member], win.at[8 * (1 - core) + member], (beyond_g, x), 4).start()
        near_copy(win.at[4 + member], win.at[8 * core + member], (partner_g, x), 5).start()

    pass_on(x)

    def arrived(ref, sem):
        pltpu.make_async_copy(ref, ref, sem).wait()

    loads[3].wait()
    acc[...] = jnp.dot(win[4 + x], tiles[0, 0], preferred_element_type=F32)
    loads[2].wait()
    loads[4].wait()

    arrived(abuf, a_recv)
    rows = flat(abuf[...])
    steps = []
    for _ in range(5):
        half = rows.shape[0] // 2
        rows = rounded(mul(rows[:half], trans[0]) + mul(rows[half:], trans[1]))
        steps.append(rows)
    at = 0
    for part in steps[1:]:
        blocks = part.shape[0] // ROWS
        tree[at : at + blocks] = part.reshape(blocks, ROWS, part.shape[1]).astype(BF16)
        at += blocks

    def send_plane(j, carry):
        pltpu.make_async_remote_copy(
            src_ref=tree.at[14], dst_ref=planes.at[z], send_sem=z_send.at[0], recv_sem=z_recv.at[0],
            device_id=(((z + j) % DEPTH) * PLANE + gp, x), device_id_type=MESH,
        ).start()
        return carry

    lax.fori_loop(1, DEPTH, send_plane, 0)
    pltpu.make_async_copy(tree.at[14], planes.at[z], z_recv.at[0]).start()
    for side, step in ((0, 1), (1, DEPTH - 1)):
        pltpu.make_async_remote_copy(
            src_ref=tree.at[0:14], dst_ref=near_z.at[side], send_sem=z_send.at[1 + side],
            recv_sem=z_recv.at[1 + side],
            device_id=(((z + step) % DEPTH) * PLANE + gp, x), device_id_type=MESH,
        ).start()
    for side, step in ((0, 2), (1, DEPTH - 2)):
        pltpu.make_async_remote_copy(
            src_ref=tree.at[12:14], dst_ref=quad_z.at[side], send_sem=z_send.at[3 + side],
            recv_sem=z_recv.at[3 + side],
            device_id=(((z + step) % DEPTH) * PLANE + gp, x), device_id_type=MESH,
        ).start()

    half_rows = win.shape[1] // 2
    arrived(win.at[4 + x_down], n_recv.at[0])
    arrived(win.at[4 + x_up], n_recv.at[1])
    near_copy(
        win.at[4 + x_down, 0:half_rows], win.at[4 + x_down, 0:half_rows], (g, x_up), 2
    ).start()
    near_copy(
        win.at[4 + x_up, half_rows : 2 * half_rows], win.at[4 + x_up, half_rows : 2 * half_rows], (g, x_down), 3
    ).start()
    pass_on(x_down)
    pass_on(x_up)

    def flag(level, pick, index, valid):
        return mask_ref[level, pick, index].astype(F32) * jnp.where(valid, 1.0, 0.0)

    def couple(level, sources):
        total = 0.0
        for pick in range(2):
            ahead, behind = sources(pick)
            total = total + mul(ahead, coup[level, pick]) + mul_t(behind, coup[level, pick])
        return total

    inside_low, inside_high = z > 0, z < DEPTH - 1

    def low_level(level, blocks, start, bits, far_low, far_high):
        def fetch(place):
            if 0 <= place < blocks:
                return tree[start + reversed_bits(place, bits)], True
            if -blocks <= place < 0:
                return near_z[0, start + reversed_bits(place + blocks, bits)], z >= 1
            if blocks <= place < 2 * blocks:
                return near_z[1, start + reversed_bits(place - blocks, bits)], z < DEPTH - 1
            if place < -blocks:
                return far_low(place + 2 * blocks), z >= 2
            return far_high(place - 2 * blocks), z < DEPTH - 2

        def sources(pick):
            offset = pick + 2
            ahead, behind = [], []
            for slot in range(blocks):
                place = reversed_bits(slot, bits)
                block, valid = fetch(place + offset)
                ahead.append(block.astype(F32) * flag(level, pick, z * blocks + place, valid))
                block, valid = fetch(place - offset)
                index = (z * blocks + place - offset + DEPTH * blocks) % (DEPTH * blocks)
                behind.append(block.astype(F32) * flag(level, pick, index, valid))
            return jnp.concatenate(ahead, axis=0), jnp.concatenate(behind, axis=0)

        return couple(level, sources)

    for side in range(2):
        arrived(near_z.at[side], z_recv.at[1 + side])
        arrived(quad_z.at[side], z_recv.at[3 + side])
    coupled0 = low_level(0, 8, 0, 3, None, None)
    coupled1 = low_level(1, 4, 8, 2, None, None)
    coupled2 = low_level(2, 2, 12, 1, lambda q: quad_z[0, q], lambda q: quad_z[1, q])

    arrived(win.at[4 + (x + 2) % MEMBERS, 0:half_rows], n_recv.at[2])
    arrived(win.at[4 + (x + 2) % MEMBERS, half_rows : 2 * half_rows], n_recv.at[3])
    pass_on((x + 2) % MEMBERS)

    arrived(planes, z_recv.at[0])

    def join(ref, count):
        lower = jnp.concatenate([ref[2 * k].astype(F32) for k in range(count)], axis=0)
        upper = jnp.concatenate([ref[2 * k + 1].astype(F32) for k in range(count)], axis=0)
        return rounded(mul(lower, trans[0]) + mul(upper, trans[1]))

    lev4[...] = join(planes, 8).reshape(lev4.shape)
    lev5[...] = join(lev4, 4).reshape(lev5.shape)

    def high_level(level, ref, count, here):
        def sources(pick):
            offset = pick + 2
            ahead = ref[(here + offset) % count].astype(F32) * flag(level, pick, here, here + offset < count)
            index = (here + count - offset) % count
            behind = ref[index].astype(F32) * flag(level, pick, index, here >= offset)
            return ahead, behind

        return couple(level, sources)

    coupled3 = high_level(3, planes, DEPTH, z)
    coupled4 = high_level(4, lev4, DEPTH // 2, z // 2)
    coupled5 = high_level(5, lev5, DEPTH // 4, z // 4)

    field = mul_t(coupled5, trans[(z // 2) % 2]) + coupled4
    field = mul_t(field, trans[z % 2]) + coupled3
    for coupled in (coupled2, coupled1, coupled0):
        field = jnp.concatenate([mul_t(field, trans[0]), mul_t(field, trans[1])], axis=0) + coupled
    fbuf[...] = field.reshape(fbuf.shape).astype(BF16)

    def send_d(j, carry):
        other = (me + j) % PEERS
        pltpu.make_async_remote_copy(
            src_ref=fbuf.at[reversed_bits(other // MEMBERS, 3)],
            dst_ref=gbuf.at[me],
            send_sem=d_send,
            recv_sem=d_recv,
            device_id=(base_g + other // MEMBERS, other % MEMBERS),
            device_id_type=MESH,
        ).start()
        return carry

    lax.fori_loop(1, PEERS, send_d, 0)
    pltpu.make_async_copy(fbuf.at[reversed_bits(gp, 3)], gbuf.at[me], d_recv).start()

    arrived(win.at[pl.ds(8 * core, 4)], n_recv.at[4])
    arrived(win.at[pl.ds(8 * (1 - core), 4)], n_recv.at[5])
    live = count_ref[0]
    leaf_low = (g - 1) * MEMBERS

    def weight(slot, col):
        leaf = leaf_low + col
        good = (leaf >= 0) & (leaf < PLANE * DEPTH * MEMBERS) & (slot < live)
        return jnp.where(good, 1.0, 0.0)

    slot_cols = (4 + x, 3 + x, 5 + x, cols_ref[0, 3])
    for slot in range(1, 4):
        col = slot_cols[slot]
        product = jnp.dot(win[col], tiles[0, slot], preferred_element_type=F32)
        acc[...] = acc[...] + weight(slot, col) * product

    arrived(gbuf, d_recv)
    field = flat(gbuf[...])
    field = mul_t(field, trans[x // 2])
    field = mul_t(field, trans[x % 2])
    out_ref[...] = (acc[...] + mul_t(field, basis[0])).astype(out_ref.dtype)

    arrived(cbuf.at[0 : PEERS - 1], a_send)
    arrived(gbuf.at[0 : PEERS - 1], d_send)
    arrived(planes.at[0 : DEPTH - 1], z_send.at[0])
    for side in range(2):
        arrived(near_z.at[side], z_send.at[1 + side])
        arrived(quad_z.at[side], z_send.at[3 + side])
    arrived(win.at[0:11], n_send)


def per_device(points_x, leaf_basis, near_tiles, near_cols, near_count, transfer, coupling, couple_mask):
    vectors, points = points_x.shape
    rank = leaf_basis.shape[2]
    hbm = pl.BlockSpec(memory_space=pl.ANY)
    smem = pl.BlockSpec(memory_space=pltpu.SMEM)
    block = (ROWS, rank)
    dma = pltpu.SemaphoreType.DMA
    return pl.pallas_call(
        kernel,
        out_shape=jax.ShapeDtypeStruct((vectors, points), BF16),
        in_specs=[hbm] * 5 + [smem] * 3,
        out_specs=pl.BlockSpec(memory_space=pltpu.VMEM),
        scratch_shapes=[
            pltpu.VMEM((12, vectors, points), BF16),
            pltpu.VMEM(leaf_basis.shape, BF16),
            pltpu.VMEM(near_tiles.shape, BF16),
            pltpu.VMEM(transfer.shape, BF16),
            pltpu.VMEM(coupling.shape, BF16),
            pltpu.VMEM((PEERS,) + block, BF16),
            pltpu.VMEM((PEERS,) + block, BF16),
            pltpu.VMEM((16,) + block, BF16),
            pltpu.VMEM((2, 14) + block, BF16),
            pltpu.VMEM((2, 2) + block, BF16),
            pltpu.VMEM((DEPTH,) + block, BF16),
            pltpu.VMEM((DEPTH // 2,) + block, F32),
            pltpu.VMEM((DEPTH // 4,) + block, F32),
            pltpu.VMEM((PLANE,) + block, BF16),
            pltpu.VMEM((PEERS,) + block, BF16),
            pltpu.VMEM((vectors, points), F32),
            dma((5,)), dma(()), dma(()), dma((5,)), dma((5,)), dma(()), dma(()), dma(()), dma((6,)),
        ],
        compiler_params=pltpu.CompilerParams(
            collective_id=0, has_side_effects=True, vmem_limit_bytes=48 * 1024 * 1024
        ),
    )(
        points_x, leaf_basis, near_tiles, transfer, coupling,
        near_cols, near_count, jnp.transpose(couple_mask, (0, 2, 1)),
    )


def solution(mesh):
    in_specs = (
        P(None, ("leaf", "level")),
        P(("leaf", "level"), None, None),
        P(("leaf", "level"), None, None, None),
        P(("leaf", "level"), None),
        P(("leaf", "level")),
        P(),
        P(),
        P(),
    )
    out_specs = P(None, ("leaf", "level"))
    return jax.shard_map(per_device, mesh=mesh, in_specs=in_specs, out_specs=out_specs, check_vma=False)
```

```python
import jax
import jax.numpy as jnp
from jax import lax
from jax.experimental import pallas as pl
from jax.experimental.pallas import tpu as pltpu
from jax.sharding import PartitionSpec as P

MESH = pl.DeviceIdType.MESH
F32, BF16 = jnp.float32, jnp.bfloat16

PLANE = 8
MEMBERS = 4
PEERS = PLANE * MEMBERS
DEPTH = 16
GROUPS = PLANE * DEPTH
ROWS = 8
EARLY = 6
SEL, EDGE = 8, 9

REACH = (0, 1, 2, 1)
PEER_STEPS = sorted(
    ((dx, dy, dc) for dx in range(4) for dy in range(4) for dc in range(2) if (dx, dy, dc) != (0, 0, 0)),
    key=lambda s: -(REACH[s[0]] + REACH[s[1]]),
)
DEPTH_STEPS = sorted(range(1, DEPTH), key=lambda s: -min(s, DEPTH - s))


def flat(blocks):
    wide = blocks.astype(F32)
    return wide.reshape(wide.shape[0] * wide.shape[1], wide.shape[2])


def mul(rows, matrix):
    return jnp.dot(rows.astype(BF16), matrix, preferred_element_type=F32)


def mul_t(rows, matrix):
    return lax.dot_general(
        rows.astype(BF16), matrix, (((1,), (1,)), ((), ())), preferred_element_type=F32
    )


def rounded(rows):
    return rows.astype(BF16).astype(F32)


def piece(rows, index):
    return rows[ROWS * index : ROWS * (index + 1)]


def kernel(
    count_ref, x_hbm, basis_hbm, tiles_hbm, transfer_hbm, coupling_hbm, cols_hbm, mask_hbm,
    out_ref,
    win, basis, tiles, trans, coup, mask_ref, cols_ref,
    cbuf, abuf, tree, near_z, quad_z, planes, fbuf, gbuf, acc, low,
    two, three, ahead_mats, behind_mats, ask, asked, chosen,
    load_sem, a_send, a_recv, z_send, z_recv, d_send, d_recv, n_send, n_recv, above_sem,
):
    g = lax.axis_index("leaf")
    x = lax.axis_index("level")
    z = g // PLANE
    gp = g % PLANE
    core = g % 2
    y = gp // 2
    base_g = g - gp
    me = gp * MEMBERS + x
    rank = trans.shape[2]
    partner_g = g + 1 - 2 * core
    beyond_g = (g + 2 * core - 1 + GROUPS) % GROUPS
    has_beyond = (g > 0) & (g < GROUPS - 1)
    at_edge = x == core * (MEMBERS - 1)
    x_up, x_down, x_far = (x + 1) % MEMBERS, (x + 3) % MEMBERS, (x + 2) % MEMBERS

    def load(k, src, dst):
        return pltpu.make_async_copy(src, dst, load_sem.at[k])

    load_x = load(0, x_hbm, win.at[x])
    load_basis = load(1, basis_hbm, basis)
    load_trans = load(2, transfer_hbm, trans)
    load_cols = load(3, cols_hbm, cols_ref)
    load_mask = load(4, mask_hbm, mask_ref)
    load_coup = load(5, coupling_hbm, coup)
    load_tiles = load(6, tiles_hbm, tiles)
    for item in (load_basis, load_trans, load_x, load_cols, load_mask, load_coup, load_tiles):
        item.start()

    def plane_peer(step):
        dx, dy, dc = step
        other_core = 1 - core if dc else core
        other_y = (y + dy) % 4
        return other_y * 2 + other_core, (x + dx) % MEMBERS

    def z_peer(step):
        return ((z + step) % DEPTH) * PLANE + gp, x

    barrier = pltpu.get_barrier_semaphore()

    def greet_above(plane, carry):
        pl.semaphore_signal(barrier, inc=1, device_id=(plane * PLANE + gp, x), device_id_type=MESH)
        return carry

    lax.fori_loop(z + 1, DEPTH, greet_above, 0)
    for step in PEER_STEPS:
        other_gp, other_x = plane_peer(step)
        pl.semaphore_signal(barrier, inc=1, device_id=(base_g + other_gp, other_x), device_id_type=MESH)
    edge_x = (MEMBERS - 1) * (1 - core)

    @pl.when(has_beyond)
    def _():
        pl.semaphore_signal(barrier, inc=1, device_id=(beyond_g, x), device_id_type=MESH)

    @pl.when(has_beyond & at_edge)
    def _():
        pl.semaphore_signal(barrier, inc=1, device_id=(beyond_g, edge_x), device_id_type=MESH)

    def arrived(ref, sem):
        pltpu.make_async_copy(ref, ref, sem).wait()

    load_trans.wait()
    load_basis.wait()
    up = mul(basis[0], trans[x % 2])
    basis[0] = mul(up, trans[x // 2]).astype(BF16)
    load_x.wait()
    coef = jnp.dot(win[x], basis[0], preferred_element_type=F32)
    cbuf[...] = coef.reshape(PEERS, ROWS, rank).astype(BF16)

    @pl.when(jnp.logical_not(has_beyond))
    def _():
        win[SEL] = jnp.zeros(win.shape[1:], BF16)
        win[EDGE] = jnp.zeros(win.shape[1:], BF16)

    load_cols.wait()
    extra = cols_ref[0, 3]
    wanted = jnp.where(core == 0, extra, extra - 2 * MEMBERS)
    ask[...] = jnp.broadcast_to(wanted.astype(F32), ask.shape)

    greeted = PEERS - 1 + z + jnp.where(has_beyond, 1, 0) + jnp.where(has_beyond & at_edge, 1, 0)
    pl.semaphore_wait(barrier, greeted)

    def greet_below(plane, carry):
        pl.semaphore_signal(above_sem, inc=1, device_id=(plane * PLANE + gp, x), device_id_type=MESH)
        return carry

    lax.fori_loop(0, z, greet_below, 0)

    def near_copy(src, dst, where, send, recv):
        return pltpu.make_async_remote_copy(
            src_ref=src, dst_ref=dst, send_sem=n_send.at[send], recv_sem=n_recv.at[recv],
            device_id=where, device_id_type=MESH,
        )

    ask_copy = near_copy(ask, asked, (beyond_g, x), 3, 7)

    @pl.when(has_beyond)
    def _():
        ask_copy.start()

    half = win.shape[1] // 2

    def first(place):
        return win.at[place, 0:half]

    def last(place):
        return win.at[place, half : 2 * half]

    def share():
        near_copy(first(x), first(x), (g, x_up), 0, 0).start()
        near_copy(last(x), last(x), (g, x_down), 0, 1).start()
        near_copy(last(x), last(x), (g, x_up), 0, 8).start()
        near_copy(first(x), first(x), (g, x_down), 0, 9).start()
        near_copy(win.at[x], win.at[4 + x], (partner_g, x), 0, 4).start()

    my_slot = x * PLANE + gp
    for step in PEER_STEPS:
        other_gp, other_x = plane_peer(step)
        pltpu.make_async_remote_copy(
            src_ref=cbuf.at[other_gp * MEMBERS + other_x], dst_ref=abuf.at[my_slot],
            send_sem=a_send, recv_sem=a_recv,
            device_id=(base_g + other_gp, other_x), device_id_type=MESH,
        ).start()
    pltpu.make_async_copy(cbuf.at[me], abuf.at[my_slot], a_recv).start()

    @pl.when(z < EARLY)
    def _():
        share()

    both = trans[...].reshape(2 * rank, rank)
    for upper in range(2):
        two[2 * rank * upper : 2 * rank * (upper + 1)] = mul(both, trans[upper]).astype(BF16)
    for upper in range(2):
        three[4 * rank * upper : 4 * rank * (upper + 1)] = mul(two[...], trans[upper]).astype(BF16)

    sel_copy = near_copy(chosen, win.at[SEL], (beyond_g, x), 1, 5)
    edge_copy = near_copy(win.at[x], win.at[EDGE], (beyond_g, edge_x), 2, 6)
    sends_edge = has_beyond & at_edge
    lanes = ask.shape[1]

    def relay():
        arrived(first(x_down), n_recv.at[0])
        near_copy(first(x_down), first(x_down), (g, x_up), 0, 2).start()
        arrived(last(x_up), n_recv.at[1])
        near_copy(last(x_up), last(x_up), (g, x_down), 0, 3).start()
        arrived(last(x_down), n_recv.at[8])
        arrived(first(x_up), n_recv.at[9])
        near_copy(win.at[x_down], win.at[4 + x_down], (partner_g, x), 0, 4).start()
        near_copy(win.at[x_up], win.at[4 + x_up], (partner_g, x), 0, 4).start()

    def relay_far():
        arrived(first(x_far), n_recv.at[2])
        arrived(last(x_far), n_recv.at[3])
        near_copy(win.at[x_far], win.at[4 + x_far], (partner_g, x), 0, 4).start()

        @pl.when(has_beyond)
        def _():
            arrived(asked, n_recv.at[7])
            tile = asked[...]
            for at in range(0, win.shape[2], lanes):
                total = 0.0
                for member in range(MEMBERS):
                    part = win[member, :, at : at + lanes].astype(F32)
                    part = part.reshape(part.shape[0] // ask.shape[0], ask.shape[0], lanes)
                    total = total + part * jnp.where(tile == member, 1.0, 0.0)[None]
                chosen[:, at : at + lanes] = total.reshape(chosen.shape[0], lanes).astype(BF16)
            sel_copy.start()

        @pl.when(sends_edge)
        def _():
            edge_copy.start()

    arrived(abuf, a_recv)
    rows = flat(abuf[...])
    share_rows = PLANE * ROWS
    tops = rounded(sum(rows[share_rows * k : share_rows * (k + 1)] for k in range(MEMBERS)))
    in_line = jnp.concatenate([piece(tops, k) for k in range(PLANE)], axis=1)
    tree[14] = mul(in_line, three[...]).astype(BF16)

    @pl.when(z < EARLY)
    def _():
        relay()

    @pl.when(z < DEPTH - 1)
    def _():
        pl.semaphore_wait(above_sem, DEPTH - 1 - z)

    for step in DEPTH_STEPS:
        pltpu.make_async_remote_copy(
            src_ref=tree.at[14], dst_ref=planes.at[z], send_sem=z_send.at[0], recv_sem=z_recv.at[0],
            device_id=z_peer(step), device_id_type=MESH,
        ).start()
    pltpu.make_async_copy(tree.at[14], planes.at[z], z_recv.at[0]).start()

    def join(parts):
        count = parts.shape[0] // (2 * ROWS)
        lower = jnp.concatenate([piece(parts, 2 * k) for k in range(count)], axis=0)
        upper = jnp.concatenate([piece(parts, 2 * k + 1) for k in range(count)], axis=0)
        return rounded(mul(lower, trans[0]) + mul(upper, trans[1]))

    pairs = join(tops)
    quads = join(pairs)
    at = 0
    for part in (tops, pairs, quads):
        blocks = part.shape[0] // ROWS
        tree[at : at + blocks] = part.reshape(blocks, ROWS, rank).astype(BF16)
        at += blocks
    for side, step in ((0, 1), (1, DEPTH - 1)):
        pltpu.make_async_remote_copy(
            src_ref=tree.at[0:14], dst_ref=near_z.at[side], send_sem=z_send.at[1 + side],
            recv_sem=z_recv.at[1 + side], device_id=z_peer(step), device_id_type=MESH,
        ).start()
    for side, step in ((0, 2), (1, DEPTH - 2)):
        pltpu.make_async_remote_copy(
            src_ref=tree.at[12:14], dst_ref=quad_z.at[side], send_sem=z_send.at[3 + side],
            recv_sem=z_recv.at[3 + side], device_id=z_peer(step), device_id_type=MESH,
        ).start()

    @pl.when(z >= EARLY)
    def _():
        share()

    load_coup.wait()
    down_two = two[pl.ds(pl.multiple_of((z % 4) * rank, rank), rank), :]
    down_one = trans[z % 2]
    for pick in range(2):
        for place, level, down in ((pick, 5, down_two), (2 + pick, 4, down_one)):
            matrix = coup[level, pick]
            at = rank * place
            ahead_mats[at : at + rank, :] = mul_t(matrix, down).astype(BF16)
            behind_mats[:, at : at + rank] = mul(down, matrix).astype(BF16)
        at = rank * (4 + pick)
        ahead_mats[at : at + rank, :] = coup[3, pick]
        behind_mats[:, at : at + rank] = coup[3, pick]

    load_tiles.wait()
    acc[...] = jnp.dot(win[x], tiles[0, 0], preferred_element_type=F32)

    @pl.when(z >= EARLY)
    def _():
        relay()

    relay_far()
    load_mask.wait()

    def flag(level, pick, index, valid):
        return mask_ref[level, pick, index].astype(F32) * jnp.where(valid, 1.0, 0.0)

    def low_level(level, blocks, start):
        def fetch(place):
            if 0 <= place < blocks:
                return tree[start + place], True
            if -blocks <= place < 0:
                return near_z[0, start + place + blocks], z >= 1
            if blocks <= place < 2 * blocks:
                return near_z[1, start + place - blocks], z < DEPTH - 1
            if place < -blocks:
                return quad_z[0, place + 2 * blocks], z >= 2
            return quad_z[1, place - 2 * blocks], z < DEPTH - 2

        total = 0.0
        for pick in range(2):
            offset = pick + 2
            ahead, behind = [], []
            for place in range(blocks):
                block, valid = fetch(place + offset)
                ahead.append(block.astype(F32) * flag(level, pick, z * blocks + place, valid))
                block, valid = fetch(place - offset)
                index = (z * blocks + place - offset + DEPTH * blocks) % (DEPTH * blocks)
                behind.append(block.astype(F32) * flag(level, pick, index, valid))
            total = total + mul(jnp.concatenate(ahead, axis=0), coup[level, pick])
            total = total + mul_t(jnp.concatenate(behind, axis=0), coup[level, pick])
        return total

    def split(parents):
        lower, upper = mul_t(parents, trans[0]), mul_t(parents, trans[1])
        parts = []
        for k in range(parents.shape[0] // ROWS):
            parts += [piece(lower, k), piece(upper, k)]
        return jnp.concatenate(parts, axis=0)

    for side in range(2):
        arrived(near_z.at[side], z_recv.at[1 + side])
        arrived(quad_z.at[side], z_recv.at[3 + side])
    low[...] = split(split(low_level(2, 2, 12)) + low_level(1, 4, 8)) + low_level(0, 8, 0)

    arrived(planes, z_recv.at[0])
    pair, quad = z // 2, z // 4
    steps = (2, 3, -2, -3)

    def gathered(count, here, index):
        return jnp.concatenate(
            [planes[index((here + step + count) % count)].astype(F32) for step in steps], axis=0
        )

    level5 = sum(
        mul(gathered(4, quad, lambda k, r=r: 4 * k + r), two[rank * r : rank * (r + 1)]) for r in range(4)
    )
    level4 = sum(mul(gathered(8, pair, lambda k, r=r: 2 * k + r), trans[r]) for r in range(2))
    level3 = gathered(DEPTH, z, lambda k: k)

    def flagged(level, rows, count, here):
        ahead, behind = [], []
        for pick in range(2):
            offset = pick + 2
            ahead.append(piece(rows, pick) * flag(level, pick, here, here + offset < count))
            index = (here + count - offset) % count
            behind.append(piece(rows, 2 + pick) * flag(level, pick, index, here >= offset))
        return ahead, behind

    ahead, behind = [], []
    for level, rows, count, here in (
        (5, rounded(level5), 4, quad), (4, rounded(level4), 8, pair), (3, level3, DEPTH, z),
    ):
        one, other = flagged(level, rows, count, here)
        ahead += one
        behind += other
    field = mul(jnp.concatenate(ahead, axis=1), ahead_mats[...])
    field = field + mul_t(jnp.concatenate(behind, axis=1), behind_mats[...])
    spread = mul_t(field, three[...])
    spread = jnp.concatenate([spread[:, rank * k : rank * (k + 1)] for k in range(PLANE)], axis=0)
    fbuf[...] = (spread + low[...]).reshape(fbuf.shape).astype(BF16)

    for step in PEER_STEPS:
        other_gp, other_x = plane_peer(step)
        pltpu.make_async_remote_copy(
            src_ref=fbuf.at[other_gp], dst_ref=gbuf.at[me], send_sem=d_send, recv_sem=d_recv,
            device_id=(base_g + other_gp, other_x), device_id_type=MESH,
        ).start()
    pltpu.make_async_copy(fbuf.at[gp], gbuf.at[me], d_recv).start()

    arrived(win.at[4:8], n_recv.at[4])

    @pl.when(sends_edge)
    def _():
        arrived(win.at[EDGE], n_recv.at[6])

    before = jnp.where(x > 0, x - 1, jnp.where(core == 1, 7, EDGE))
    after = jnp.where(x < MEMBERS - 1, x + 1, jnp.where(core == 0, 4, EDGE))
    acc[...] = (
        acc[...]
        + jnp.dot(win[before], tiles[0, 1], preferred_element_type=F32)
        + jnp.dot(win[after], tiles[0, 2], preferred_element_type=F32)
    )

    @pl.when(has_beyond)
    def _():
        arrived(win.at[SEL], n_recv.at[5])

    low_col, high_col = extra < MEMBERS, extra >= 2 * MEMBERS
    if_first = jnp.where(low_col, SEL, extra - MEMBERS)
    if_second = jnp.where(high_col, SEL, jnp.where(low_col, extra + MEMBERS, extra - MEMBERS))
    place = jnp.where(core == 0, if_first, if_second)
    weight = jnp.where(count_ref[0] > 3, 1.0, 0.0)
    acc[...] = acc[...] + weight * jnp.dot(win[place], tiles[0, 3], preferred_element_type=F32)

    arrived(gbuf, d_recv)
    out_ref[...] = (acc[...] + mul_t(flat(gbuf[...]), basis[0])).astype(out_ref.dtype)

    arrived(cbuf.at[0 : PEERS - 1], a_send)
    arrived(gbuf.at[0 : PEERS - 1], d_send)
    arrived(planes.at[0 : DEPTH - 1], z_send.at[0])
    for side in range(2):
        arrived(near_z.at[side], z_send.at[1 + side])
        arrived(quad_z.at[side], z_send.at[3 + side])
    arrived(win.at[0:7], n_send.at[0])

    @pl.when(has_beyond)
    def _():
        arrived(ask, n_send.at[3])
        arrived(chosen, n_send.at[1])

    @pl.when(sends_edge)
    def _():
        arrived(win.at[EDGE], n_send.at[2])


def per_device(points_x, leaf_basis, near_tiles, near_cols, near_count, transfer, coupling, couple_mask):
    vectors, points = points_x.shape
    rank = leaf_basis.shape[2]
    masks = jnp.transpose(couple_mask, (0, 2, 1))
    operands = (points_x, leaf_basis, near_tiles, transfer, coupling, near_cols, masks)
    hbm = pl.BlockSpec(memory_space=pltpu.HBM)
    block = (ROWS, rank)
    dma = pltpu.SemaphoreType.DMA
    return pl.pallas_call(
        kernel,
        out_shape=jax.ShapeDtypeStruct((vectors, points), BF16),
        in_specs=[pl.BlockSpec(memory_space=pltpu.SMEM)] + [hbm] * 7,
        out_specs=pl.BlockSpec(memory_space=pltpu.VMEM),
        scratch_shapes=[
            pltpu.VMEM((10, vectors, points), BF16),
            pltpu.VMEM(leaf_basis.shape, BF16),
            pltpu.VMEM(near_tiles.shape, BF16),
            pltpu.VMEM(transfer.shape, BF16),
            pltpu.VMEM(coupling.shape, BF16),
            pltpu.SMEM(masks.shape, jnp.int32),
            pltpu.SMEM(near_cols.shape, jnp.int32),
            pltpu.VMEM((PEERS,) + block, BF16),
            pltpu.VMEM((PEERS,) + block, BF16),
            pltpu.VMEM((15,) + block, BF16),
            pltpu.VMEM((2, 14) + block, BF16),
            pltpu.VMEM((2, 2) + block, BF16),
            pltpu.VMEM((DEPTH,) + block, BF16),
            pltpu.VMEM((PLANE,) + block, BF16),
            pltpu.VMEM((PEERS,) + block, BF16),
            pltpu.VMEM((vectors, points), F32),
            pltpu.VMEM((PLANE * ROWS, rank), F32),
            pltpu.VMEM((4 * rank, rank), BF16),
            pltpu.VMEM((8 * rank, rank), BF16),
            pltpu.VMEM((6 * rank, rank), BF16),
            pltpu.VMEM((rank, 6 * rank), BF16),
            pltpu.VMEM((8, 128), F32),
            pltpu.VMEM((8, 128), F32),
            pltpu.VMEM((vectors, points), BF16),
            dma((7,)), dma(()), dma(()), dma((5,)), dma((5,)), dma(()), dma(()), dma((4,)), dma((10,)), pltpu.SemaphoreType.REGULAR,
        ],
        compiler_params=pltpu.CompilerParams(
            collective_id=0, has_side_effects=True, vmem_limit_bytes=48 * 1024 * 1024
        ),
    )(near_count, *(pltpu.with_memory_space_constraint(a, pltpu.HBM) for a in operands))


def solution(mesh):
    in_specs = (
        P(None, ("leaf", "level")),
        P(("leaf", "level"), None, None),
        P(("leaf", "level"), None, None, None),
        P(("leaf", "level"), None),
        P(("leaf", "level")),
        P(),
        P(),
        P(),
    )
    out_specs = P(None, ("leaf", "level"))
    return jax.shard_map(per_device, mesh=mesh, in_specs=in_specs, out_specs=out_specs, check_vma=False)
```

```python
import jax
import jax.numpy as jnp
from jax import lax
from jax.experimental import pallas as pl
from jax.experimental.pallas import tpu as pltpu
from jax.sharding import PartitionSpec as P

MESH = pl.DeviceIdType.MESH
F32, BF16 = jnp.float32, jnp.bfloat16

PLANE = 8
MEMBERS = 4
PEERS = PLANE * MEMBERS
DEPTH = 16
GROUPS = PLANE * DEPTH
ROWS = 8
EARLY = 5
SEL, EDGE = 8, 9

REACH = (0, 1, 2, 1)
PEER_STEPS = sorted(
    ((dx, dy, dc) for dx in range(4) for dy in range(4) for dc in range(2) if (dx, dy, dc) != (0, 0, 0)),
    key=lambda s: -(REACH[s[0]] + REACH[s[1]]),
)


def flat(blocks):
    wide = blocks.astype(F32)
    return wide.reshape(wide.shape[0] * wide.shape[1], wide.shape[2])


def mul(rows, matrix):
    return jnp.dot(rows.astype(BF16), matrix, preferred_element_type=F32)


def mul_t(rows, matrix):
    return lax.dot_general(
        rows.astype(BF16), matrix, (((1,), (1,)), ((), ())), preferred_element_type=F32
    )


def rounded(rows):
    return rows.astype(BF16).astype(F32)


def piece(rows, index):
    return rows[ROWS * index : ROWS * (index + 1)]


def kernel(
    count_ref, x_hbm, basis_hbm, tiles_hbm, transfer_hbm, coupling_hbm, cols_hbm, mask_hbm,
    out_ref,
    win, basis, tiles, trans, coup, mask_ref, cols_ref,
    cbuf, abuf, tree, near_z, quad_z, planes, fbuf, gbuf, lbuf, lows, acc, plane_basis,
    two, three, ahead_mats, behind_mats, ask, asked, chosen,
    load_sem, a_send, a_recv, z_send, z_recv, d_send, d_recv, l_send, l_recv, n_send, n_recv, above_sem, next_sem,
):
    g = lax.axis_index("leaf")
    x = lax.axis_index("level")
    z = g // PLANE
    gp = g % PLANE
    core = g % 2
    y = gp // 2
    base_g = g - gp
    me = gp * MEMBERS + x
    rank = trans.shape[2]
    partner_g = g + 1 - 2 * core
    beyond_g = (g + 2 * core - 1 + GROUPS) % GROUPS
    has_beyond = (g > 0) & (g < GROUPS - 1)
    edge_x = core * (MEMBERS - 1)
    wants_edge = has_beyond & (x == edge_x)
    sends_edge = has_beyond & (x == MEMBERS - 1 - edge_x)
    x_up, x_down, x_far = (x + 1) % MEMBERS, (x + 3) % MEMBERS, (x + 2) % MEMBERS

    def load(k, src, dst):
        return pltpu.make_async_copy(src, dst, load_sem.at[k])

    load_x = load(0, x_hbm, win.at[x])
    load_basis = load(1, basis_hbm, basis)
    load_trans = load(2, transfer_hbm, trans)
    load_cols = load(3, cols_hbm, cols_ref)
    load_mask = load(4, mask_hbm, mask_ref)
    load_coup = load(5, coupling_hbm, coup)
    load_tiles = load(6, tiles_hbm, tiles)
    for item in (load_basis, load_trans, load_x, load_cols, load_mask, load_coup, load_tiles):
        item.start()

    def plane_peer(step):
        dx, dy, dc = step
        other_core = 1 - core if dc else core
        other_y = (y + dy) % 4
        return other_y * 2 + other_core, (x + dx) % MEMBERS

    def z_peer(step):
        return ((z + step) % DEPTH) * PLANE + gp, x

    barrier = pltpu.get_barrier_semaphore()

    def greet_above(plane, carry):
        pl.semaphore_signal(barrier, inc=1, device_id=(plane * PLANE + gp, x), device_id_type=MESH)
        return carry

    lax.fori_loop(z + 1, DEPTH, greet_above, 0)
    for step in PEER_STEPS:
        other_gp, other_x = plane_peer(step)
        pl.semaphore_signal(barrier, inc=1, device_id=(base_g + other_gp, other_x), device_id_type=MESH)

    @pl.when(has_beyond)
    def _():
        pl.semaphore_signal(barrier, inc=1, device_id=(beyond_g, x), device_id_type=MESH)

    def arrived(ref, sem):
        pltpu.make_async_copy(ref, ref, sem).wait()

    load_trans.wait()
    load_basis.wait()
    up = mul(basis[0], trans[x % 2])
    basis[0] = mul(up, trans[x // 2]).astype(BF16)
    load_x.wait()
    coef = jnp.dot(win[x], basis[0], preferred_element_type=F32)
    cbuf[...] = coef.reshape(PEERS, ROWS, rank).astype(BF16)

    @pl.when(jnp.logical_not(has_beyond))
    def _():
        win[SEL] = jnp.zeros(win.shape[1:], BF16)
        win[EDGE] = jnp.zeros(win.shape[1:], BF16)

    for distance, far in ((1, near_z), (2, quad_z)):

        @pl.when(z < distance)
        def _():
            far[0] = jnp.zeros(far.shape[1:], BF16)

        @pl.when(z >= DEPTH - distance)
        def _():
            far[1] = jnp.zeros(far.shape[1:], BF16)

    load_cols.wait()
    extra = cols_ref[0, 3]
    wanted = jnp.where(core == 0, extra, extra - 2 * MEMBERS)
    ask[...] = jnp.broadcast_to(wanted.astype(F32), ask.shape)

    greeted = PEERS - 1 + z + jnp.where(has_beyond, 1, 0)
    pl.semaphore_wait(barrier, greeted)

    def greet_below(plane, carry):
        pl.semaphore_signal(above_sem, inc=1, device_id=(plane * PLANE + gp, x), device_id_type=MESH)
        return carry

    lax.fori_loop(0, z, greet_below, 0)
    for distance in (1, 2):

        @pl.when(z >= distance)
        def _():
            pl.semaphore_signal(next_sem.at[distance - 1], inc=1, device_id=(g - distance * PLANE, x), device_id_type=MESH)

    def near_copy(src, dst, where, send, recv):
        return pltpu.make_async_remote_copy(
            src_ref=src, dst_ref=dst, send_sem=n_send.at[send], recv_sem=n_recv.at[recv],
            device_id=where, device_id_type=MESH,
        )

    ask_copy = near_copy(ask, asked, (beyond_g, x), 3, 7)

    @pl.when(has_beyond)
    def _():
        ask_copy.start()

    half = win.shape[1] // 2

    def first(place):
        return win.at[place, 0:half]

    def last(place):
        return win.at[place, half : 2 * half]

    def share():
        near_copy(first(x), first(x), (g, x_up), 0, 0).start()
        near_copy(last(x), last(x), (g, x_down), 0, 1).start()
        near_copy(last(x), last(x), (g, x_up), 0, 8).start()
        near_copy(first(x), first(x), (g, x_down), 0, 9).start()
        near_copy(win.at[x], win.at[4 + x], (partner_g, x), 0, 4).start()

    my_slot = x * PLANE + gp
    for step in PEER_STEPS:
        other_gp, other_x = plane_peer(step)
        pltpu.make_async_remote_copy(
            src_ref=cbuf.at[other_gp * MEMBERS + other_x], dst_ref=abuf.at[my_slot],
            send_sem=a_send, recv_sem=a_recv,
            device_id=(base_g + other_gp, other_x), device_id_type=MESH,
        ).start()
    pltpu.make_async_copy(cbuf.at[me], abuf.at[my_slot], a_recv).start()

    @pl.when(z < EARLY)
    def _():
        share()

    both = trans[...].reshape(2 * rank, rank)
    for upper in range(2):
        two[2 * rank * upper : 2 * rank * (upper + 1)] = mul(both, trans[upper]).astype(BF16)
    for upper in range(2):
        three[4 * rank * upper : 4 * rank * (upper + 1)] = mul(two[...], trans[upper]).astype(BF16)

    sel_copy = near_copy(chosen, win.at[SEL], (beyond_g, x), 1, 5)
    edge_copy = near_copy(win.at[edge_x], win.at[EDGE], (beyond_g, x), 2, 6)
    lanes = ask.shape[1]

    def relay():
        arrived(first(x_down), n_recv.at[0])
        near_copy(first(x_down), first(x_down), (g, x_up), 0, 2).start()
        arrived(last(x_up), n_recv.at[1])
        near_copy(last(x_up), last(x_up), (g, x_down), 0, 3).start()
        arrived(last(x_down), n_recv.at[8])
        arrived(first(x_up), n_recv.at[9])

        @pl.when(sends_edge)
        def _():
            edge_copy.start()

        near_copy(win.at[x_down], win.at[4 + x_down], (partner_g, x), 0, 4).start()
        near_copy(win.at[x_up], win.at[4 + x_up], (partner_g, x), 0, 4).start()

    def relay_far():
        arrived(first(x_far), n_recv.at[2])
        arrived(last(x_far), n_recv.at[3])
        near_copy(win.at[x_far], win.at[4 + x_far], (partner_g, x), 0, 4).start()

        @pl.when(has_beyond)
        def _():
            arrived(asked, n_recv.at[7])
            tile = asked[...]
            for at in range(0, win.shape[2], lanes):
                total = 0.0
                for member in range(MEMBERS):
                    part = win[member, :, at : at + lanes].astype(F32)
                    part = part.reshape(part.shape[0] // ask.shape[0], ask.shape[0], lanes)
                    total = total + part * jnp.where(tile == member, 1.0, 0.0)[None]
                chosen[:, at : at + lanes] = total.reshape(chosen.shape[0], lanes).astype(BF16)
            sel_copy.start()

    arrived(abuf, a_recv)
    rows = flat(abuf[...])
    share_rows = PLANE * ROWS
    tops = rounded(sum(rows[share_rows * k : share_rows * (k + 1)] for k in range(MEMBERS)))
    in_line = jnp.concatenate([piece(tops, k) for k in range(PLANE)], axis=1)
    tree[14] = mul(in_line, three[...]).astype(BF16)

    def send_plane(plane, carry):
        pltpu.make_async_remote_copy(
            src_ref=tree.at[14], dst_ref=planes.at[z], send_sem=z_send.at[0], recv_sem=z_recv.at[0],
            device_id=(plane * PLANE + gp, x), device_id_type=MESH,
        ).start()
        return carry

    lax.fori_loop(0, z, send_plane, 0)
    pltpu.make_async_copy(tree.at[14], planes.at[z], z_recv.at[0]).start()

    @pl.when(z >= EARLY)
    def _():
        share()

    def join(parts):
        count = parts.shape[0] // (2 * ROWS)
        lower = jnp.concatenate([piece(parts, 2 * k) for k in range(count)], axis=0)
        upper = jnp.concatenate([piece(parts, 2 * k + 1) for k in range(count)], axis=0)
        return rounded(mul(lower, trans[0]) + mul(upper, trans[1]))

    pairs = join(tops)
    quads = join(pairs)
    at = 0
    for part in (tops, pairs, quads):
        blocks = part.shape[0] // ROWS
        tree[at : at + blocks] = part.reshape(blocks, ROWS, rank).astype(BF16)
        at += blocks

    def send_tree(side, step, blocks, target, k):
        return pltpu.make_async_remote_copy(
            src_ref=blocks, dst_ref=target.at[side], send_sem=z_send.at[k + side],
            recv_sem=z_recv.at[k + side], device_id=z_peer(step), device_id_type=MESH,
        )

    tree_up, tree_down = (send_tree(k, s, tree.at[0:14], near_z, 1) for k, s in ((0, 1), (1, DEPTH - 1)))
    quad_up, quad_down = (send_tree(k, s, tree.at[12:14], quad_z, 3) for k, s in ((0, 2), (1, DEPTH - 2)))

    @pl.when(z >= 1)
    def _():
        tree_down.start()

    @pl.when(z >= 2)
    def _():
        quad_down.start()

    load_coup.wait()
    down_two = two[pl.ds(pl.multiple_of((z % 4) * rank, rank), rank), :]
    down_one = trans[z % 2]
    for pick in range(2):
        for place, level, down in ((pick, 5, down_two), (2 + pick, 4, down_one)):
            matrix = coup[level, pick]
            at = rank * place
            ahead_mats[at : at + rank, :] = mul_t(matrix, down).astype(BF16)
            behind_mats[:, at : at + rank] = mul(down, matrix).astype(BF16)
        at = rank * (4 + pick)
        ahead_mats[at : at + rank, :] = coup[3, pick]
        behind_mats[:, at : at + rank] = coup[3, pick]

    plane_basis[...] = mul(basis[0], three[pl.ds(pl.multiple_of(gp * rank, rank), rank), :]).astype(BF16)

    load_tiles.wait()
    acc[...] = jnp.dot(win[x], tiles[0, 0], preferred_element_type=F32)

    @pl.when(z < EARLY)
    def _():
        relay()

    for distance, copy in ((1, tree_up), (2, quad_up)):

        @pl.when(z < DEPTH - distance)
        def _():
            pl.semaphore_wait(next_sem.at[distance - 1], 1)
            copy.start()

    def reach_above():
        @pl.when(z < DEPTH - 1)
        def _():
            pl.semaphore_wait(above_sem, DEPTH - 1 - z)

        lax.fori_loop(z + 1, DEPTH, send_plane, 0)

    @pl.when(z >= EARLY)
    def _():
        reach_above()
        relay()

    load_mask.wait()

    def flag(level, pick, index, valid):
        return mask_ref[level, pick, index].astype(F32) * jnp.where(valid, 1.0, 0.0)

    def low_level(level, blocks, start):
        def fetch(place):
            if 0 <= place < blocks:
                return tree[start + place], True
            if -blocks <= place < 0:
                return near_z[0, start + place + blocks], z >= 1
            if blocks <= place < 2 * blocks:
                return near_z[1, start + place - blocks], z < DEPTH - 1
            if place < -blocks:
                return quad_z[0, place + 2 * blocks], z >= 2
            return quad_z[1, place - 2 * blocks], z < DEPTH - 2

        total = 0.0
        for pick in range(2):
            offset = pick + 2
            ahead, behind = [], []
            for place in range(blocks):
                block, valid = fetch(place + offset)
                ahead.append(block.astype(F32) * flag(level, pick, z * blocks + place, valid))
                block, valid = fetch(place - offset)
                index = (z * blocks + place - offset + DEPTH * blocks) % (DEPTH * blocks)
                behind.append(block.astype(F32) * flag(level, pick, index, valid))
            total = total + mul(jnp.concatenate(ahead, axis=0), coup[level, pick])
            total = total + mul_t(jnp.concatenate(behind, axis=0), coup[level, pick])
        return total

    def split(parents):
        lower, upper = mul_t(parents, trans[0]), mul_t(parents, trans[1])
        parts = []
        for k in range(parents.shape[0] // ROWS):
            parts += [piece(lower, k), piece(upper, k)]
        return jnp.concatenate(parts, axis=0)

    for distance, far, k in ((1, near_z, 1), (2, quad_z, 3)):

        @pl.when(z >= distance)
        def _():
            arrived(far.at[0], z_recv.at[k])

        @pl.when(z < DEPTH - distance)
        def _():
            arrived(far.at[1], z_recv.at[k + 1])

    low = split(split(low_level(2, 2, 12)) + low_level(1, 4, 8)) + low_level(0, 8, 0)
    lbuf[...] = low.reshape(lbuf.shape).astype(BF16)
    for step in PEER_STEPS:
        other_gp, other_x = plane_peer(step)
        pltpu.make_async_remote_copy(
            src_ref=lbuf.at[other_gp], dst_ref=lows.at[me], send_sem=l_send, recv_sem=l_recv,
            device_id=(base_g + other_gp, other_x), device_id_type=MESH,
        ).start()
    pltpu.make_async_copy(lbuf.at[gp], lows.at[me], l_recv).start()

    @pl.when(z < EARLY)
    def _():
        reach_above()

    relay_far()

    arrived(planes, z_recv.at[0])
    pair, quad = z // 2, z // 4
    steps = (2, 3, -2, -3)

    def gathered(count, here, index):
        return jnp.concatenate(
            [planes[index((here + step + count) % count)].astype(F32) for step in steps], axis=0
        )

    level5 = sum(
        mul(gathered(4, quad, lambda k, r=r: 4 * k + r), two[rank * r : rank * (r + 1)]) for r in range(4)
    )
    level4 = sum(mul(gathered(8, pair, lambda k, r=r: 2 * k + r), trans[r]) for r in range(2))
    level3 = gathered(DEPTH, z, lambda k: k)

    def flagged(level, rows, count, here):
        ahead, behind = [], []
        for pick in range(2):
            offset = pick + 2
            ahead.append(piece(rows, pick) * flag(level, pick, here, here + offset < count))
            index = (here + count - offset) % count
            behind.append(piece(rows, 2 + pick) * flag(level, pick, index, here >= offset))
        return ahead, behind

    ahead, behind = [], []
    for level, rows, count, here in (
        (5, rounded(level5), 4, quad), (4, rounded(level4), 8, pair), (3, level3, DEPTH, z),
    ):
        one, other = flagged(level, rows, count, here)
        ahead += one
        behind += other
    field = mul(jnp.concatenate(ahead, axis=1), ahead_mats[...])
    field = field + mul_t(jnp.concatenate(behind, axis=1), behind_mats[...])
    fbuf[...] = field.astype(BF16)

    for step in PEER_STEPS:
        other_gp, other_x = plane_peer(step)
        pltpu.make_async_remote_copy(
            src_ref=fbuf, dst_ref=gbuf.at[me], send_sem=d_send, recv_sem=d_recv,
            device_id=(base_g + other_gp, other_x), device_id_type=MESH,
        ).start()
    pltpu.make_async_copy(fbuf, gbuf.at[me], d_recv).start()

    arrived(win.at[4:8], n_recv.at[4])

    @pl.when(wants_edge)
    def _():
        arrived(win.at[EDGE], n_recv.at[6])

    before = jnp.where(x > 0, x - 1, jnp.where(core == 1, 7, EDGE))
    after = jnp.where(x < MEMBERS - 1, x + 1, jnp.where(core == 0, 4, EDGE))
    acc[...] = (
        acc[...]
        + jnp.dot(win[before], tiles[0, 1], preferred_element_type=F32)
        + jnp.dot(win[after], tiles[0, 2], preferred_element_type=F32)
    )

    @pl.when(has_beyond)
    def _():
        arrived(win.at[SEL], n_recv.at[5])

    low_col, high_col = extra < MEMBERS, extra >= 2 * MEMBERS
    if_first = jnp.where(low_col, SEL, extra - MEMBERS)
    if_second = jnp.where(high_col, SEL, jnp.where(low_col, extra + MEMBERS, extra - MEMBERS))
    place = jnp.where(core == 0, if_first, if_second)
    weight = jnp.where(count_ref[0] > 3, 1.0, 0.0)
    acc[...] = acc[...] + weight * jnp.dot(win[place], tiles[0, 3], preferred_element_type=F32)

    arrived(lows, l_recv)
    acc[...] = acc[...] + mul_t(flat(lows[...]), basis[0])

    arrived(gbuf, d_recv)
    out_ref[...] = (acc[...] + mul_t(flat(gbuf[...]), plane_basis[...])).astype(out_ref.dtype)

    arrived(cbuf.at[0 : PEERS - 1], a_send)
    arrived(gbuf.at[0 : PEERS - 1], d_send)
    arrived(lows.at[0 : PEERS - 1], l_send)
    arrived(planes.at[0 : DEPTH - 1], z_send.at[0])
    for distance, far, k in ((1, near_z, 1), (2, quad_z, 3)):

        @pl.when(z < DEPTH - distance)
        def _():
            arrived(far.at[0], z_send.at[k])

        @pl.when(z >= distance)
        def _():
            arrived(far.at[1], z_send.at[k + 1])

    arrived(win.at[0:7], n_send.at[0])

    @pl.when(has_beyond)
    def _():
        arrived(ask, n_send.at[3])
        arrived(chosen, n_send.at[1])

    @pl.when(sends_edge)
    def _():
        arrived(win.at[EDGE], n_send.at[2])


def per_device(points_x, leaf_basis, near_tiles, near_cols, near_count, transfer, coupling, couple_mask):
    vectors, points = points_x.shape
    rank = leaf_basis.shape[2]
    masks = jnp.transpose(couple_mask, (0, 2, 1))
    operands = (points_x, leaf_basis, near_tiles, transfer, coupling, near_cols, masks)
    hbm = pl.BlockSpec(memory_space=pltpu.HBM)
    block = (ROWS, rank)
    dma = pltpu.SemaphoreType.DMA
    return pl.pallas_call(
        kernel,
        out_shape=jax.ShapeDtypeStruct((vectors, points), BF16),
        in_specs=[pl.BlockSpec(memory_space=pltpu.SMEM)] + [hbm] * 7,
        out_specs=pl.BlockSpec(memory_space=pltpu.VMEM),
        scratch_shapes=[
            pltpu.VMEM((10, vectors, points), BF16),
            pltpu.VMEM(leaf_basis.shape, BF16),
            pltpu.VMEM(near_tiles.shape, BF16),
            pltpu.VMEM(transfer.shape, BF16),
            pltpu.VMEM(coupling.shape, BF16),
            pltpu.SMEM(masks.shape, jnp.int32),
            pltpu.SMEM(near_cols.shape, jnp.int32),
            pltpu.VMEM((PEERS,) + block, BF16),
            pltpu.VMEM((PEERS,) + block, BF16),
            pltpu.VMEM((15,) + block, BF16),
            pltpu.VMEM((2, 14) + block, BF16),
            pltpu.VMEM((2, 2) + block, BF16),
            pltpu.VMEM((DEPTH,) + block, BF16),
            pltpu.VMEM(block, BF16),
            pltpu.VMEM((PEERS,) + block, BF16),
            pltpu.VMEM((PLANE,) + block, BF16),
            pltpu.VMEM((PEERS,) + block, BF16),
            pltpu.VMEM((vectors, points), F32),
            pltpu.VMEM((points, rank), BF16),
            pltpu.VMEM((4 * rank, rank), BF16),
            pltpu.VMEM((8 * rank, rank), BF16),
            pltpu.VMEM((6 * rank, rank), BF16),
            pltpu.VMEM((rank, 6 * rank), BF16),
            pltpu.VMEM((8, 128), F32),
            pltpu.VMEM((8, 128), F32),
            pltpu.VMEM((vectors, points), BF16),
            dma((7,)), dma(()), dma(()), dma((5,)), dma((5,)), dma(()), dma(()), dma(()), dma(()), dma((4,)), dma((10,)), pltpu.SemaphoreType.REGULAR,
            pltpu.SemaphoreType.REGULAR((2,)),
        ],
        compiler_params=pltpu.CompilerParams(
            collective_id=0, has_side_effects=True, vmem_limit_bytes=48 * 1024 * 1024
        ),
    )(near_count, *(pltpu.with_memory_space_constraint(a, pltpu.HBM) for a in operands))


def solution(mesh):
    in_specs = (
        P(None, ("leaf", "level")),
        P(("leaf", "level"), None, None),
        P(("leaf", "level"), None, None, None),
        P(("leaf", "level"), None),
        P(("leaf", "level")),
        P(),
        P(),
        P(),
    )
    out_specs = P(None, ("leaf", "level"))
    return jax.shard_map(per_device, mesh=mesh, in_specs=in_specs, out_specs=out_specs, check_vma=False)
```

```python
import jax
import jax.numpy as jnp
from jax import lax
from jax.experimental import pallas as pl
from jax.experimental.pallas import tpu as pltpu
from jax.sharding import PartitionSpec as P

MESH = pl.DeviceIdType.MESH
F32, BF16 = jnp.float32, jnp.bfloat16

PLANE = 8
MEMBERS = 4
PEERS = PLANE * MEMBERS
DEPTH = 16
GROUPS = PLANE * DEPTH
ROWS = 8
EARLY = 5
SEL, EDGE = 8, 9

REACH = (0, 1, 2, 1)
PEER_STEPS = sorted(
    ((dx, dy, dc) for dx in range(4) for dy in range(4) for dc in range(2) if (dx, dy, dc) != (0, 0, 0)),
    key=lambda s: -(REACH[s[0]] + REACH[s[1]]),
)


def flat(blocks):
    wide = blocks.astype(F32)
    return wide.reshape(wide.shape[0] * wide.shape[1], wide.shape[2])


def mul(rows, matrix):
    return jnp.dot(rows.astype(BF16), matrix, preferred_element_type=F32)


def mul_t(rows, matrix):
    return lax.dot_general(
        rows.astype(BF16), matrix, (((1,), (1,)), ((), ())), preferred_element_type=F32
    )


def rounded(rows):
    return rows.astype(BF16).astype(F32)


def piece(rows, index):
    return rows[ROWS * index : ROWS * (index + 1)]


def kernel(
    count_ref, x_hbm, basis_hbm, tiles_hbm, transfer_hbm, coupling_hbm, cols_hbm, mask_hbm,
    out_ref,
    win, basis, tiles, trans, coup, mask_ref, cols_ref,
    cbuf, abuf, tree, near_z, quad_z, planes, fbuf, gbuf, lbuf, lows, acc, plane_basis,
    two, three, ahead_mats, behind_mats, ask, asked, chosen,
    load_sem, a_send, a_recv, z_send, z_recv, d_send, d_recv, l_send, l_recv, n_send, n_recv, above_sem, next_sem,
):
    g = lax.axis_index("leaf")
    x = lax.axis_index("level")
    z = g // PLANE
    gp = g % PLANE
    core = g % 2
    y = gp // 2
    base_g = g - gp
    me = gp * MEMBERS + x
    rank = trans.shape[2]
    partner_g = g + 1 - 2 * core
    beyond_g = (g + 2 * core - 1 + GROUPS) % GROUPS
    has_beyond = (g > 0) & (g < GROUPS - 1)
    edge_x = core * (MEMBERS - 1)
    wants_edge = has_beyond & (x == edge_x)
    sends_edge = has_beyond & (x == MEMBERS - 1 - edge_x)
    x_up, x_down, x_far = (x + 1) % MEMBERS, (x + 3) % MEMBERS, (x + 2) % MEMBERS

    def load(k, src, dst):
        return pltpu.make_async_copy(src, dst, load_sem.at[k])

    load_x = load(0, x_hbm, win.at[x])
    load_basis = load(1, basis_hbm, basis)
    load_trans = load(2, transfer_hbm, trans)
    load_cols = load(3, cols_hbm, cols_ref)
    load_mask = load(4, mask_hbm, mask_ref)
    load_coup = load(5, coupling_hbm, coup)
    load_tiles = load(6, tiles_hbm, tiles)
    for item in (load_basis, load_trans, load_x, load_cols, load_mask, load_coup, load_tiles):
        item.start()

    def plane_peer(step):
        dx, dy, dc = step
        other_core = 1 - core if dc else core
        other_y = (y + dy) % 4
        return other_y * 2 + other_core, (x + dx) % MEMBERS

    def z_peer(step):
        return ((z + step) % DEPTH) * PLANE + gp, x

    barrier = pltpu.get_barrier_semaphore()

    def greet_above(plane, carry):
        pl.semaphore_signal(barrier, inc=1, device_id=(plane * PLANE + gp, x), device_id_type=MESH)
        return carry

    lax.fori_loop(z + 1, DEPTH, greet_above, 0)
    for step in PEER_STEPS:
        other_gp, other_x = plane_peer(step)
        pl.semaphore_signal(barrier, inc=1, device_id=(base_g + other_gp, other_x), device_id_type=MESH)

    @pl.when(has_beyond)
    def _():
        pl.semaphore_signal(barrier, inc=1, device_id=(beyond_g, x), device_id_type=MESH)

    def arrived(ref, sem):
        pltpu.make_async_copy(ref, ref, sem).wait()

    load_trans.wait()
    load_basis.wait()
    up = mul(basis[0], trans[x % 2])
    basis[0] = mul(up, trans[x // 2]).astype(BF16)
    load_x.wait()
    coef = jnp.dot(win[x], basis[0], preferred_element_type=F32)
    cbuf[...] = coef.reshape(PEERS, ROWS, rank).astype(BF16)

    @pl.when(jnp.logical_not(has_beyond))
    def _():
        win[SEL] = jnp.zeros(win.shape[1:], BF16)
        win[EDGE] = jnp.zeros(win.shape[1:], BF16)

    for distance, far in ((1, near_z), (2, quad_z)):

        @pl.when(z < distance)
        def _():
            far[0] = jnp.zeros(far.shape[1:], BF16)

        @pl.when(z >= DEPTH - distance)
        def _():
            far[1] = jnp.zeros(far.shape[1:], BF16)

    load_cols.wait()
    extra = cols_ref[0, 3]
    wanted = jnp.where(core == 0, extra, extra - 2 * MEMBERS)
    ask[...] = jnp.broadcast_to(wanted.astype(F32), ask.shape)

    greeted = PEERS - 1 + z + jnp.where(has_beyond, 1, 0)
    pl.semaphore_wait(barrier, greeted)

    def greet_below(plane, carry):
        pl.semaphore_signal(above_sem, inc=1, device_id=(plane * PLANE + gp, x), device_id_type=MESH)
        return carry

    lax.fori_loop(0, z, greet_below, 0)
    for distance in (1, 2):

        @pl.when(z >= distance)
        def _():
            pl.semaphore_signal(next_sem.at[distance - 1], inc=1, device_id=(g - distance * PLANE, x), device_id_type=MESH)

    def near_copy(src, dst, where, send, recv):
        return pltpu.make_async_remote_copy(
            src_ref=src, dst_ref=dst, send_sem=n_send.at[send], recv_sem=n_recv.at[recv],
            device_id=where, device_id_type=MESH,
        )

    ask_copy = near_copy(ask, asked, (beyond_g, x), 3, 7)

    @pl.when(has_beyond)
    def _():
        ask_copy.start()

    half = win.shape[1] // 2

    def first(place):
        return win.at[place, 0:half]

    def last(place):
        return win.at[place, half : 2 * half]

    def share():
        near_copy(first(x), first(x), (g, x_up), 0, 0).start()
        near_copy(last(x), last(x), (g, x_down), 0, 1).start()
        near_copy(last(x), last(x), (g, x_up), 0, 8).start()
        near_copy(first(x), first(x), (g, x_down), 0, 9).start()
        near_copy(win.at[x], win.at[4 + x], (partner_g, x), 0, 4).start()

    my_slot = x * PLANE + gp
    for step in PEER_STEPS:
        other_gp, other_x = plane_peer(step)
        pltpu.make_async_remote_copy(
            src_ref=cbuf.at[other_gp * MEMBERS + other_x], dst_ref=abuf.at[my_slot],
            send_sem=a_send, recv_sem=a_recv,
            device_id=(base_g + other_gp, other_x), device_id_type=MESH,
        ).start()
    pltpu.make_async_copy(cbuf.at[me], abuf.at[my_slot], a_recv).start()

    @pl.when(z < EARLY)
    def _():
        share()

    both = trans[...].reshape(2 * rank, rank)
    for upper in range(2):
        two[2 * rank * upper : 2 * rank * (upper + 1)] = mul(both, trans[upper]).astype(BF16)
    for upper in range(2):
        three[4 * rank * upper : 4 * rank * (upper + 1)] = mul(two[...], trans[upper]).astype(BF16)

    sel_copy = near_copy(chosen, win.at[SEL], (beyond_g, x), 1, 5)
    edge_copy = near_copy(win.at[edge_x], win.at[EDGE], (beyond_g, x), 2, 6)
    lanes = ask.shape[1]

    def relay():
        arrived(first(x_down), n_recv.at[0])
        near_copy(first(x_down), first(x_down), (g, x_up), 0, 2).start()
        arrived(last(x_up), n_recv.at[1])
        near_copy(last(x_up), last(x_up), (g, x_down), 0, 3).start()
        arrived(last(x_down), n_recv.at[8])
        arrived(first(x_up), n_recv.at[9])

        @pl.when(sends_edge)
        def _():
            edge_copy.start()

        near_copy(win.at[x_down], win.at[4 + x_down], (partner_g, x), 0, 4).start()
        near_copy(win.at[x_up], win.at[4 + x_up], (partner_g, x), 0, 4).start()

    def relay_far():
        arrived(first(x_far), n_recv.at[2])
        arrived(last(x_far), n_recv.at[3])
        near_copy(win.at[x_far], win.at[4 + x_far], (partner_g, x), 0, 4).start()

        @pl.when(has_beyond)
        def _():
            arrived(asked, n_recv.at[7])
            tile = asked[...]
            for at in range(0, win.shape[2], lanes):
                total = 0.0
                for member in range(MEMBERS):
                    part = win[member, :, at : at + lanes].astype(F32)
                    part = part.reshape(part.shape[0] // ask.shape[0], ask.shape[0], lanes)
                    total = total + part * jnp.where(tile == member, 1.0, 0.0)[None]
                chosen[:, at : at + lanes] = total.reshape(chosen.shape[0], lanes).astype(BF16)
            sel_copy.start()

    arrived(abuf, a_recv)
    rows = flat(abuf[...])
    share_rows = PLANE * ROWS
    tops = rounded(sum(rows[share_rows * k : share_rows * (k + 1)] for k in range(MEMBERS)))
    in_line = jnp.concatenate([piece(tops, k) for k in range(PLANE)], axis=1)
    tree[14] = mul(in_line, three[...]).astype(BF16)

    def send_plane(plane, carry):
        pltpu.make_async_remote_copy(
            src_ref=tree.at[14], dst_ref=planes.at[z], send_sem=z_send.at[0], recv_sem=z_recv.at[0],
            device_id=(plane * PLANE + gp, x), device_id_type=MESH,
        ).start()
        return carry

    lax.fori_loop(0, z, send_plane, 0)
    pltpu.make_async_copy(tree.at[14], planes.at[z], z_recv.at[0]).start()

    @pl.when(z >= EARLY)
    def _():
        share()

    def join(parts):
        count = parts.shape[0] // (2 * ROWS)
        lower = jnp.concatenate([piece(parts, 2 * k) for k in range(count)], axis=0)
        upper = jnp.concatenate([piece(parts, 2 * k + 1) for k in range(count)], axis=0)
        return rounded(mul(lower, trans[0]) + mul(upper, trans[1]))

    pairs = join(tops)
    quads = join(pairs)
    at = 0
    for part in (tops, pairs, quads):
        blocks = part.shape[0] // ROWS
        tree[at : at + blocks] = part.reshape(blocks, ROWS, rank).astype(BF16)
        at += blocks

    def send_tree(side, step, blocks, target, k):
        return pltpu.make_async_remote_copy(
            src_ref=blocks, dst_ref=target.at[side], send_sem=z_send.at[k + side],
            recv_sem=z_recv.at[k + side], device_id=z_peer(step), device_id_type=MESH,
        )

    tree_up, tree_down = (send_tree(k, s, tree.at[0:14], near_z, 1) for k, s in ((0, 1), (1, DEPTH - 1)))
    quad_up, quad_down = (send_tree(k, s, tree.at[12:14], quad_z, 3) for k, s in ((0, 2), (1, DEPTH - 2)))

    @pl.when(z >= 1)
    def _():
        tree_down.start()

    @pl.when(z >= 2)
    def _():
        quad_down.start()

    load_coup.wait()
    down_two = two[pl.ds(pl.multiple_of((z % 4) * rank, rank), rank), :]
    down_one = trans[z % 2]
    for pick in range(2):
        for place, level, down in ((pick, 5, down_two), (2 + pick, 4, down_one)):
            matrix = coup[level, pick]
            at = rank * place
            ahead_mats[at : at + rank, :] = mul_t(matrix, down).astype(BF16)
            behind_mats[:, at : at + rank] = mul(down, matrix).astype(BF16)
        at = rank * (4 + pick)
        ahead_mats[at : at + rank, :] = coup[3, pick]
        behind_mats[:, at : at + rank] = coup[3, pick]

    plane_basis[...] = mul(basis[0], three[pl.ds(pl.multiple_of(gp * rank, rank), rank), :]).astype(BF16)

    load_tiles.wait()
    acc[...] = jnp.dot(win[x], tiles[0, 0], preferred_element_type=F32)

    @pl.when(z < EARLY)
    def _():
        relay()

    for distance, copy in ((1, tree_up), (2, quad_up)):

        @pl.when(z < DEPTH - distance)
        def _():
            pl.semaphore_wait(next_sem.at[distance - 1], 1)
            copy.start()

    def reach_above():
        @pl.when(z < DEPTH - 1)
        def _():
            pl.semaphore_wait(above_sem, DEPTH - 1 - z)

        lax.fori_loop(z + 1, DEPTH, send_plane, 0)

    @pl.when(z >= EARLY)
    def _():
        reach_above()
        relay()
        relay_far()

    load_mask.wait()

    def flag(level, pick, index, valid):
        return mask_ref[level, pick, index].astype(F32) * jnp.where(valid, 1.0, 0.0)

    def low_level(level, blocks, start):
        def fetch(place):
            if 0 <= place < blocks:
                return tree[start + place], True
            if -blocks <= place < 0:
                return near_z[0, start + place + blocks], z >= 1
            if blocks <= place < 2 * blocks:
                return near_z[1, start + place - blocks], z < DEPTH - 1
            if place < -blocks:
                return quad_z[0, place + 2 * blocks], z >= 2
            return quad_z[1, place - 2 * blocks], z < DEPTH - 2

        total = 0.0
        for pick in range(2):
            offset = pick + 2
            ahead, behind = [], []
            for place in range(blocks):
                block, valid = fetch(place + offset)
                ahead.append(block.astype(F32) * flag(level, pick, z * blocks + place, valid))
                block, valid = fetch(place - offset)
                index = (z * blocks + place - offset + DEPTH * blocks) % (DEPTH * blocks)
                behind.append(block.astype(F32) * flag(level, pick, index, valid))
            total = total + mul(jnp.concatenate(ahead, axis=0), coup[level, pick])
            total = total + mul_t(jnp.concatenate(behind, axis=0), coup[level, pick])
        return total

    def split(parents):
        lower, upper = mul_t(parents, trans[0]), mul_t(parents, trans[1])
        parts = []
        for k in range(parents.shape[0] // ROWS):
            parts += [piece(lower, k), piece(upper, k)]
        return jnp.concatenate(parts, axis=0)

    for distance, far, k in ((1, near_z, 1), (2, quad_z, 3)):

        @pl.when(z >= distance)
        def _():
            arrived(far.at[0], z_recv.at[k])

        @pl.when(z < DEPTH - distance)
        def _():
            arrived(far.at[1], z_recv.at[k + 1])

    low = split(split(low_level(2, 2, 12)) + low_level(1, 4, 8)) + low_level(0, 8, 0)
    lbuf[...] = low.reshape(lbuf.shape).astype(BF16)
    for step in PEER_STEPS:
        other_gp, other_x = plane_peer(step)
        pltpu.make_async_remote_copy(
            src_ref=lbuf.at[other_gp], dst_ref=lows.at[me], send_sem=l_send, recv_sem=l_recv,
            device_id=(base_g + other_gp, other_x), device_id_type=MESH,
        ).start()
    pltpu.make_async_copy(lbuf.at[gp], lows.at[me], l_recv).start()

    @pl.when(z < EARLY)
    def _():
        reach_above()
        relay_far()


    arrived(planes, z_recv.at[0])
    pair, quad = z // 2, z // 4
    steps = (2, 3, -2, -3)

    def gathered(count, here, index):
        return jnp.concatenate(
            [planes[index((here + step + count) % count)].astype(F32) for step in steps], axis=0
        )

    level5 = sum(
        mul(gathered(4, quad, lambda k, r=r: 4 * k + r), two[rank * r : rank * (r + 1)]) for r in range(4)
    )
    level4 = sum(mul(gathered(8, pair, lambda k, r=r: 2 * k + r), trans[r]) for r in range(2))
    level3 = gathered(DEPTH, z, lambda k: k)

    def flagged(level, rows, count, here):
        ahead, behind = [], []
        for pick in range(2):
            offset = pick + 2
            ahead.append(piece(rows, pick) * flag(level, pick, here, here + offset < count))
            index = (here + count - offset) % count
            behind.append(piece(rows, 2 + pick) * flag(level, pick, index, here >= offset))
        return ahead, behind

    ahead, behind = [], []
    for level, rows, count, here in (
        (5, rounded(level5), 4, quad), (4, rounded(level4), 8, pair), (3, level3, DEPTH, z),
    ):
        one, other = flagged(level, rows, count, here)
        ahead += one
        behind += other
    field = mul(jnp.concatenate(ahead, axis=1), ahead_mats[...])
    field = field + mul_t(jnp.concatenate(behind, axis=1), behind_mats[...])
    fbuf[...] = field.astype(BF16)

    for step in PEER_STEPS:
        other_gp, other_x = plane_peer(step)
        pltpu.make_async_remote_copy(
            src_ref=fbuf, dst_ref=gbuf.at[me], send_sem=d_send, recv_sem=d_recv,
            device_id=(base_g + other_gp, other_x), device_id_type=MESH,
        ).start()
    pltpu.make_async_copy(fbuf, gbuf.at[me], d_recv).start()

    arrived(win.at[4:8], n_recv.at[4])

    @pl.when(wants_edge)
    def _():
        arrived(win.at[EDGE], n_recv.at[6])

    before = jnp.where(x > 0, x - 1, jnp.where(core == 1, 7, EDGE))
    after = jnp.where(x < MEMBERS - 1, x + 1, jnp.where(core == 0, 4, EDGE))
    acc[...] = (
        acc[...]
        + jnp.dot(win[before], tiles[0, 1], preferred_element_type=F32)
        + jnp.dot(win[after], tiles[0, 2], preferred_element_type=F32)
    )

    @pl.when(has_beyond)
    def _():
        arrived(win.at[SEL], n_recv.at[5])

    low_col, high_col = extra < MEMBERS, extra >= 2 * MEMBERS
    if_first = jnp.where(low_col, SEL, extra - MEMBERS)
    if_second = jnp.where(high_col, SEL, jnp.where(low_col, extra + MEMBERS, extra - MEMBERS))
    place = jnp.where(core == 0, if_first, if_second)
    weight = jnp.where(count_ref[0] > 3, 1.0, 0.0)
    acc[...] = acc[...] + weight * jnp.dot(win[place], tiles[0, 3], preferred_element_type=F32)

    arrived(lows, l_recv)
    acc[...] = acc[...] + mul_t(flat(lows[...]), basis[0])

    arrived(gbuf, d_recv)
    out_ref[...] = (acc[...] + mul_t(flat(gbuf[...]), plane_basis[...])).astype(out_ref.dtype)

    arrived(cbuf.at[0 : PEERS - 1], a_send)
    arrived(gbuf.at[0 : PEERS - 1], d_send)
    arrived(lows.at[0 : PEERS - 1], l_send)
    arrived(planes.at[0 : DEPTH - 1], z_send.at[0])
    for distance, far, k in ((1, near_z, 1), (2, quad_z, 3)):

        @pl.when(z < DEPTH - distance)
        def _():
            arrived(far.at[0], z_send.at[k])

        @pl.when(z >= distance)
        def _():
            arrived(far.at[1], z_send.at[k + 1])

    arrived(win.at[0:7], n_send.at[0])

    @pl.when(has_beyond)
    def _():
        arrived(ask, n_send.at[3])
        arrived(chosen, n_send.at[1])

    @pl.when(sends_edge)
    def _():
        arrived(win.at[EDGE], n_send.at[2])


def per_device(points_x, leaf_basis, near_tiles, near_cols, near_count, transfer, coupling, couple_mask):
    vectors, points = points_x.shape
    rank = leaf_basis.shape[2]
    masks = jnp.transpose(couple_mask, (0, 2, 1))
    operands = (points_x, leaf_basis, near_tiles, transfer, coupling, near_cols, masks)
    hbm = pl.BlockSpec(memory_space=pltpu.HBM)
    block = (ROWS, rank)
    dma = pltpu.SemaphoreType.DMA
    return pl.pallas_call(
        kernel,
        out_shape=jax.ShapeDtypeStruct((vectors, points), BF16),
        in_specs=[pl.BlockSpec(memory_space=pltpu.SMEM)] + [hbm] * 7,
        out_specs=pl.BlockSpec(memory_space=pltpu.VMEM),
        scratch_shapes=[
            pltpu.VMEM((10, vectors, points), BF16),
            pltpu.VMEM(leaf_basis.shape, BF16),
            pltpu.VMEM(near_tiles.shape, BF16),
            pltpu.VMEM(transfer.shape, BF16),
            pltpu.VMEM(coupling.shape, BF16),
            pltpu.SMEM(masks.shape, jnp.int32),
            pltpu.SMEM(near_cols.shape, jnp.int32),
            pltpu.VMEM((PEERS,) + block, BF16),
            pltpu.VMEM((PEERS,) + block, BF16),
            pltpu.VMEM((15,) + block, BF16),
            pltpu.VMEM((2, 14) + block, BF16),
            pltpu.VMEM((2, 2) + block, BF16),
            pltpu.VMEM((DEPTH,) + block, BF16),
            pltpu.VMEM(block, BF16),
            pltpu.VMEM((PEERS,) + block, BF16),
            pltpu.VMEM((PLANE,) + block, BF16),
            pltpu.VMEM((PEERS,) + block, BF16),
            pltpu.VMEM((vectors, points), F32),
            pltpu.VMEM((points, rank), BF16),
            pltpu.VMEM((4 * rank, rank), BF16),
            pltpu.VMEM((8 * rank, rank), BF16),
            pltpu.VMEM((6 * rank, rank), BF16),
            pltpu.VMEM((rank, 6 * rank), BF16),
            pltpu.VMEM((8, 128), F32),
            pltpu.VMEM((8, 128), F32),
            pltpu.VMEM((vectors, points), BF16),
            dma((7,)), dma(()), dma(()), dma((5,)), dma((5,)), dma(()), dma(()), dma(()), dma(()), dma((4,)), dma((10,)), pltpu.SemaphoreType.REGULAR,
            pltpu.SemaphoreType.REGULAR((2,)),
        ],
        compiler_params=pltpu.CompilerParams(
            collective_id=0, has_side_effects=True, vmem_limit_bytes=48 * 1024 * 1024
        ),
    )(near_count, *(pltpu.with_memory_space_constraint(a, pltpu.HBM) for a in operands))


def solution(mesh):
    in_specs = (
        P(None, ("leaf", "level")),
        P(("leaf", "level"), None, None),
        P(("leaf", "level"), None, None, None),
        P(("leaf", "level"), None),
        P(("leaf", "level")),
        P(),
        P(),
        P(),
    )
    out_specs = P(None, ("leaf", "level"))
    return jax.shard_map(per_device, mesh=mesh, in_specs=in_specs, out_specs=out_specs, check_vma=False)
```
